32 devices in a mesh: dp: 16 (over z, x, core), tensor: 2 (over y).
Axes of the slice: x: 2, y: 2, z: 4, core: 2. Of those that a mesh axis runs over, the one named last changes fastest.
Arguments:
- tokens: bfloat16 [16, 1568, 768], P('dp', 'tensor'), may hold values from -6 to 6
- cotangent: bfloat16 [16, 1568, 768], P('dp', 'tensor'), may hold values from -6 to 6
- time_attend: bfloat16 [768, 3, 768], P('dp', None, 'tensor'), may hold values from -0.21875 to 0.21875
- time_output: bfloat16 [768, 768], P('tensor', 'dp'), may hold values from -0.625 to 0.625
- time_mixing: bfloat16 [768, 768], P('dp'), may hold values from -0.21875 to 0.21875
- space_attend: bfloat16 [768, 3, 768], P('dp', None, 'tensor'), may hold values from -0.21875 to 0.21875
- space_output: bfloat16 [768, 768], P('tensor', 'dp'), may hold values from -0.875 to 0.875
- hidden_expand: bfloat16 [768, 3072], P('dp', 'tensor'), may hold values from -0.21875 to 0.21875
- hidden_reduce: bfloat16 [3072, 768], P('tensor', 'dp'), may hold values from -0.109375 to 0.109375
- norm_time: float32 [768], replicated, may hold values from 0.1 to 1.9
- norm_space: float32 [768], replicated, may hold values from 0.1 to 1.9
- norm_hidden: float32 [768], replicated, may hold values from 0.1 to 1.9
- timeattend_lower: bfloat16 [8, 768, 16], replicated, may hold values from -0.21875 to 0.21875
- timeattend_raise: bfloat16 [8, 16, 3, 768], replicated, may hold values from -1.5 to 1.5
- timeoutput_lower: bfloat16 [8, 768, 16], replicated, may hold values from -0.21875 to 0.21875
- timeoutput_raise: bfloat16 [8, 16, 768], replicated, may hold values from -1.5 to 1.5
- timemixing_lower: bfloat16 [8, 768, 16], replicated, may hold values from -0.21875 to 0.21875
- timemixing_raise: bfloat16 [8, 16, 768], replicated, may hold values from -1.5 to 1.5
- spaceattend_lower: bfloat16 [8, 768, 16], replicated, may hold values from -0.21875 to 0.21875
- spaceattend_raise: bfloat16 [8, 16, 3, 768], replicated, may hold values from -1.5 to 1.5
- spaceoutput_lower: bfloat16 [8, 768, 16], replicated, may hold values from -0.21875 to 0.21875
- spaceoutput_raise: bfloat16 [8, 16, 768], replicated, may hold values from -1.5 to 1.5
- expand_lower: bfloat16 [8, 768, 16], replicated, may hold values from -0.21875 to 0.21875
- expand_raise: bfloat16 [8, 16, 3072], replicated, may hold values from -1.5 to 1.5
- reduce_lower: bfloat16 [8, 3072, 16], replicated, may hold values from -0.109375 to 0.109375
- reduce_raise: bfloat16 [8, 16, 768], replicated, may hold values from -1.5 to 1.5
- adapter_index: int32 [16], P('dp'), may hold values from 0 to 7
- clip_mask: int32 [16], P('dp'), may hold values 0 or 1
Outputs:
- layer_output: bfloat16 [16, 1568, 768], P('dp', 'tensor')
- input_grad: bfloat16 [16, 1568, 768], P('dp', 'tensor')
- timeattend_lowgrad: float32 [8, 768, 16], replicated
- timeattend_raisegrad: float32 [8, 16, 3, 768], replicated
- timeoutput_lowgrad: float32 [8, 768, 16], replicated
- timeoutput_raisegrad: float32 [8, 16, 768], replicated
- timemixing_lowgrad: float32 [8, 768, 16], replicated
- timemixing_raisegrad: float32 [8, 16, 768], replicated
- spaceattend_lowgrad: float32 [8, 768, 16], replicated
- spaceattend_raisegrad: float32 [8, 16, 3, 768], replicated
- spaceoutput_lowgrad: float32 [8, 768, 16], replicated
- spaceoutput_raisegrad: float32 [8, 16, 768], replicated
- expand_lowgrad: float32 [8, 768, 16], replicated
- expand_raisegrad: float32 [8, 16, 3072], replicated
- reduce_lowgrad: float32 [8, 3072, 16], replicated
- reduce_raisegrad: float32 [8, 16, 768], replicated
The draws below stay inside these ranges and needn't reach their ends.
All inputs are finite; a program needn't handle non-finite values. No bound on the sum of `clip_mask` on one device may be relied on, other than what follows from the above.
Results may differ from the reference program's by a relative error of at most 0.04.
Values may be sent and summed in bfloat16 or wider, within the bound.
No kernel may reach another device: no remote copies, remote signals or barrier semaphores. Data moves between devices by JAX's collectives and lax.ppermute only.
A program may use at most 256 MiB of HBM per device.

```python
import jax
import jax.numpy as jnp
from jax import lax

D = 768
HEADS = 12
HEAD = 64
FF = 3072
FRAMES = 8
PLACES = 196
RANK = 16
ADAPTERS = 8
CLIP_TOK = 1568
CLIPS = 16


def touch_ends(values, key, smallest, top_value):
    spot = [jax.random.randint(jax.random.fold_in(key, axis), (), 0, length) for axis, length in enumerate(values.shape)]
    widest = values.shape.index(max(values.shape))
    beside = spot[:widest] + [(spot[widest] + 1) % values.shape[widest]] + spot[widest + 1:]
    return values.at[tuple(spot)].set(smallest).at[tuple(beside)].set(top_value)


def level_of(stream_key, shape, split, low, top_value):
    factor_of = 1.0
    for axis_at, parts in split:
        draws = jax.random.uniform(jax.random.fold_in(jax.random.fold_in(stream_key, 6), axis_at), (parts,), jnp.float32, low / len(split), top_value / len(split))
        factor_of = factor_of * jnp.repeat(jnp.exp(draws), shape[axis_at] // parts).reshape((-1,) + (1,) * (len(shape) - 1 - axis_at))
    return factor_of


def normal_values(key, dims, deviation, most, pieces=(), held_as=jnp.bfloat16):
    loudness = level_of(key, dims, pieces, -0.22, 0.18) if pieces else 1.0
    array = jax.random.normal(key, dims, jnp.float32) * deviation * loudness
    return jnp.minimum(jnp.maximum(array, -most), most).astype(held_as)


def setup_inputs(seed: int = 0) -> dict:
    splits = jax.random.split(jax.random.key(seed), 29)
    return {
        "tokens": normal_values(splits[0], (CLIPS, CLIP_TOK, D), 1.0, 6.0, ((0, 16), (1, 2))),
        "cotangent": normal_values(splits[1], (CLIPS, CLIP_TOK, D), 1.0, 6.0, ((0, 16), (1, 2))),
        "time_attend": normal_values(splits[2], (D, 3, D), D ** -0.5, 0.21875, ((0, 16), (2, 2))),
        "time_output": normal_values(splits[3], (D, D), (D // FRAMES) ** -0.5, 0.625, ((0, 2), (1, 16))),
        "time_mixing": normal_values(splits[4], (D, D), D ** -0.5, 0.21875, ((0, 16),)),
        "space_attend": normal_values(splits[5], (D, 3, D), D ** -0.5, 0.21875, ((0, 16), (2, 2))),
        "space_output": normal_values(splits[6], (D, D), (D // 16) ** -0.5, 0.875, ((0, 2), (1, 16))),
        "hidden_expand": normal_values(splits[7], (D, FF), D ** -0.5, 0.21875, ((0, 16), (1, 2))),
        "hidden_reduce": normal_values(splits[8], (FF, D), FF ** -0.5, 0.109375, ((0, 2), (1, 16))),
        "norm_time": jnp.clip(1.0 + 0.18 * jax.random.normal(splits[9], (D,), jnp.float32), 0.1, 1.9),
        "norm_space": jnp.clip(1.0 + 0.18 * jax.random.normal(splits[10], (D,), jnp.float32), 0.1, 1.9),
        "norm_hidden": jnp.clip(1.0 + 0.18 * jax.random.normal(splits[11], (D,), jnp.float32), 0.1, 1.9),
        "timeattend_lower": normal_values(splits[12], (ADAPTERS, D, RANK), D ** -0.5, 0.21875),
        "timeattend_raise": normal_values(splits[13], (ADAPTERS, RANK, 3, D), RANK ** -0.5, 1.5),
        "timeoutput_lower": normal_values(splits[14], (ADAPTERS, D, RANK), D ** -0.5, 0.21875),
        "timeoutput_raise": normal_values(splits[15], (ADAPTERS, RANK, D), RANK ** -0.5, 1.5),
        "timemixing_lower": normal_values(splits[16], (ADAPTERS, D, RANK), D ** -0.5, 0.21875),
        "timemixing_raise": normal_values(splits[17], (ADAPTERS, RANK, D), RANK ** -0.5, 1.5),
        "spaceattend_lower": normal_values(splits[18], (ADAPTERS, D, RANK), D ** -0.5, 0.21875),
        "spaceattend_raise": normal_values(splits[19], (ADAPTERS, RANK, 3, D), RANK ** -0.5, 1.5),
        "spaceoutput_lower": normal_values(splits[20], (ADAPTERS, D, RANK), D ** -0.5, 0.21875),
        "spaceoutput_raise": normal_values(splits[21], (ADAPTERS, RANK, D), RANK ** -0.5, 1.5),
        "expand_lower": normal_values(splits[22], (ADAPTERS, D, RANK), D ** -0.5, 0.21875),
        "expand_raise": normal_values(splits[23], (ADAPTERS, RANK, FF), RANK ** -0.5, 1.5),
        "reduce_lower": normal_values(splits[24], (ADAPTERS, FF, RANK), FF ** -0.5, 0.109375),
        "reduce_raise": normal_values(splits[25], (ADAPTERS, RANK, D), RANK ** -0.5, 1.5),
        "adapter_index": touch_ends(jax.random.randint(splits[26], (CLIPS,), 0, ADAPTERS), jax.random.fold_in(splits[26], 1), 0, ADAPTERS - 1).astype(jnp.int32),
        "clip_mask": touch_ends((jax.random.randint(splits[27], (CLIPS,), 0, 4) < 3).astype(jnp.int32), jax.random.fold_in(splits[27], 1), 0, 1),
    }


@jax.custom_vjp
def low(v):
    return lax.optimization_barrier(v.astype(jnp.bfloat16)).astype(jnp.float32)

@jax.custom_vjp
def low_back(v):
    return v

def low_keep(v):
    return (low(v), None)

def low_pass(kept, grad):
    return (grad,)

def back_keep(v):
    return (v, None)

def back_low(kept, grad):
    return (low(grad),)
low.defvjp(low_keep, low_pass)
low_back.defvjp(back_keep, back_low)
exact_mode = lax.Precision.HIGHEST
TIME_FORMS = ('cfphe,cgphe->cphfg', 'cphfg,cgphe->cfphe')
SPACE_FORMS = ('cfphe,cfqhe->cfhpq', 'cfhpq,cfqhe->cfphe')

def dense(left, right):
    return jnp.dot(left, right, precision=exact_mode, preferred_element_type=jnp.float32)

def layer_norm(values, gain):
    center = lax.optimization_barrier(jnp.mean(values, axis=-1, keepdims=True))
    offset = values - center
    spread = lax.optimization_barrier(jnp.mean(offset * offset, axis=-1, keepdims=True))
    return offset * lax.rsqrt(spread + 1e-06) * gain

def adapted(acts, weight, lower, raised):
    return dense(acts, weight) + dense(dense(acts, lower), raised)

def attention(packed, forms):
    packed = low_back(low(packed)).reshape(1, FRAMES, PLACES, 3, HEADS, HEAD)
    query = packed[:, :, :, 0]
    keys = packed[:, :, :, 1]
    values = packed[:, :, :, 2]
    scores = low_back(jnp.einsum(forms[0], query, keys, precision=exact_mode) * HEAD ** (-0.5))
    probs = low(jax.nn.softmax(scores, axis=-1))
    mixed = jnp.einsum(forms[1], probs, values, precision=exact_mode)
    return low_back(low(mixed.reshape(FRAMES * PLACES, HEADS * HEAD)))

def block(values, frozen, adapters, gains):

    def apply(position, acts):
        return adapted(acts, frozen[position], adapters[2 * position], adapters[2 * position + 1])
    normed = low(layer_norm(values, gains[0]))
    heads = attention(apply(0, normed), TIME_FORMS)
    merged = low_back(low(apply(1, heads)))
    after_time = values + low_back(apply(2, merged))
    normed = low(layer_norm(after_time, gains[1]))
    heads = attention(apply(3, normed), SPACE_FORMS)
    after_space = after_time + low_back(apply(4, heads))
    normed = low(layer_norm(after_space, gains[2]))
    hidden = low_back(apply(5, normed))
    active = low(jax.nn.gelu(hidden, approximate=False))
    return after_space + low_back(apply(6, active))

def reference(tokens, cotangent, time_attend, time_output, time_mixing, space_attend, space_output, hidden_expand, hidden_reduce, norm_time, norm_space, norm_hidden, timeattend_lower, timeattend_raise, timeoutput_lower, timeoutput_raise, timemixing_lower, timemixing_raise, spaceattend_lower, spaceattend_raise, spaceoutput_lower, spaceoutput_raise, expand_lower, expand_raise, reduce_lower, reduce_raise, adapter_index, clip_mask):
    frozen = (time_attend.astype(jnp.float32).reshape(D, 3 * D), time_output.astype(jnp.float32), time_mixing.astype(jnp.float32), space_attend.astype(jnp.float32).reshape(D, 3 * D), space_output.astype(jnp.float32), hidden_expand.astype(jnp.float32), hidden_reduce.astype(jnp.float32))
    gains = (norm_time.astype(jnp.float32), norm_space.astype(jnp.float32), norm_hidden.astype(jnp.float32))
    tables = (timeattend_lower, timeattend_raise.reshape(ADAPTERS, RANK, 3 * D), timeoutput_lower, timeoutput_raise, timemixing_lower, timemixing_raise, spaceattend_lower, spaceattend_raise.reshape(ADAPTERS, RANK, 3 * D), spaceoutput_lower, spaceoutput_raise, expand_lower, expand_raise, reduce_lower, reduce_raise)
    tables = tuple((table.astype(jnp.float32) for table in tables))

    def step(totals, inputs):
        clip, grad_in, index, keep = inputs
        chosen = tuple((table[index] for table in tables))
        factor = keep.astype(jnp.float32)

        def run(values, adapters):
            return block(values, frozen, adapters, gains) * factor
        result, back = jax.vjp(run, clip.astype(jnp.float32), chosen)
        clip_grad, adapter_grads = back(grad_in.astype(jnp.float32))
        totals = tuple((total.at[index].add(piece) for total, piece in zip(totals, adapter_grads)))
        return (totals, (result.astype(jnp.bfloat16), clip_grad.astype(jnp.bfloat16)))
    start = tuple((jnp.zeros_like(table) for table in tables))
    sums, (layer_output, input_grad) = lax.scan(step, start, (tokens, cotangent, adapter_index, clip_mask))
    return (layer_output, input_grad, sums[0], sums[1].reshape(ADAPTERS, RANK, 3, D), sums[2], sums[3], sums[4], sums[5], sums[6], sums[7].reshape(ADAPTERS, RANK, 3, D), sums[8], sums[9], sums[10], sums[11], sums[12], sums[13])
```

```python
from functools import partial

import jax
import jax.numpy as jnp
from jax import lax
from jax.sharding import PartitionSpec as P

HEAD = 64
PLACES = 196
BF = jnp.bfloat16
F32 = jnp.float32
ALL = ("dp", "tensor")
TIME_FORMS = ("fphe,gphe->phfg", "phfg,gphe->fphe", "phfg,fphe->gphe")
SPACE_FORMS = ("fphe,fqhe->fhpq", "fhpq,fqhe->fphe", "fhpq,fphe->fqhe")


def mm(a, b):
    return lax.dot_general(a, b, (((1,), (0,)), ((), ())), preferred_element_type=F32)


def mm_t(a, b):
    return lax.dot_general(a, b, (((1,), (1,)), ((), ())), preferred_element_type=F32)


def t_mm(a, b):
    return lax.dot_general(a, b, (((0,), (0,)), ((), ())), preferred_element_type=F32)


def layer_norm(values, gain):
    center = jnp.mean(values, axis=-1, keepdims=True)
    offset = values - center
    spread = jnp.mean(offset * offset, axis=-1, keepdims=True)
    return offset * lax.rsqrt(spread + 1e-06) * gain


def split_heads(packed, frames):
    rows, width = packed.shape
    shaped = packed.reshape(frames, rows // frames, 3, width // (3 * HEAD), HEAD)
    return (shaped[:, :, 0], shaped[:, :, 1], shaped[:, :, 2])


def attend(packed, frames, forms):
    query, keys, values = split_heads(packed, frames)
    scores = jnp.einsum(forms[0], query, keys, preferred_element_type=F32) * HEAD ** (-0.5)
    totals = jax.nn.logsumexp(scores, axis=-1, keepdims=True)
    weights = jnp.exp(scores - totals).astype(BF)
    mixed = jnp.einsum(forms[1], weights, values, preferred_element_type=F32)
    return (mixed.reshape(packed.shape[0], packed.shape[1] // 3), totals)


def attend_back(out_grad, packed, totals, frames, forms):
    query, keys, values = split_heads(packed, frames)
    grad = out_grad.reshape(query.shape)
    scale = HEAD ** (-0.5)
    scores = jnp.einsum(forms[0], query, keys, preferred_element_type=F32) * scale
    probs = jnp.exp(scores - totals)
    prob_grad = jnp.einsum(forms[0], grad, values, preferred_element_type=F32)
    value_grad = jnp.einsum(forms[2], probs.astype(BF), grad, preferred_element_type=F32)
    score_grad = probs * (prob_grad - jnp.sum(probs * prob_grad, axis=-1, keepdims=True))
    score_grad = score_grad.astype(BF)
    query_grad = jnp.einsum(forms[1], score_grad, keys, preferred_element_type=F32) * scale
    key_grad = jnp.einsum(forms[2], score_grad, query, preferred_element_type=F32) * scale
    stacked = jnp.stack((query_grad, key_grad, value_grad), axis=2)
    return stacked.reshape(packed.shape)


def body(
    tokens,
    cotangent,
    time_attend,
    time_output,
    time_mixing,
    space_attend,
    space_output,
    hidden_expand,
    hidden_reduce,
    norm_time,
    norm_space,
    norm_hidden,
    timeattend_lower,
    timeattend_raise,
    timeoutput_lower,
    timeoutput_raise,
    timemixing_lower,
    timemixing_raise,
    spaceattend_lower,
    spaceattend_raise,
    spaceoutput_lower,
    spaceoutput_raise,
    expand_lower,
    expand_raise,
    reduce_lower,
    reduce_raise,
    adapter_index,
    clip_mask,
    *,
    dp,
    tensor,
):
    me = lax.axis_index("tensor")
    devices = dp * tensor
    clips, length, width = tokens.shape
    frames = length // PLACES
    half = PLACES // tensor
    adapters, _, rank = timeattend_lower.shape
    cols = width // tensor
    units = hidden_expand.shape[1]
    adapter = adapter_index[0]
    valid = clip_mask[0].astype(F32)
    swap = [(i, (i + 1) % tensor) for i in range(tensor)]

    def slabs(matrix):
        rows = matrix.shape[0]
        return matrix.reshape(rows, -1, cols).transpose(1, 0, 2)

    mixing_cols = lax.dynamic_slice_in_dim(time_mixing, me * cols, cols, 1)
    time_pack = jnp.concatenate(
        [slabs(time_attend), slabs(time_output.T), slabs(mixing_cols)], axis=0
    )
    rest_pack = jnp.concatenate(
        [
            slabs(space_attend),
            slabs(space_output.T),
            slabs(hidden_expand),
            slabs(hidden_reduce.T),
        ],
        axis=0,
    )

    def gather(pack):
        whole = lax.all_gather(pack, ALL, axis=0, tiled=False)
        count, rows, _ = pack.shape
        whole = whole.reshape(dp, tensor, count, rows, cols).transpose(2, 0, 3, 1, 4)
        return whole.reshape(count, width, width)

    time_whole = gather(time_pack)
    rest_whole = gather(rest_pack)

    def wide(parts):
        return jnp.concatenate([parts[i] for i in range(parts.shape[0])], axis=1)

    def pick(table):
        picked = lax.dynamic_index_in_dim(table, adapter, 0, keepdims=False)
        if picked.ndim == 3:
            picked = picked.reshape(picked.shape[0], -1)
        return picked

    def regroup(table, axis):
        shape = table.shape
        pieces = units // cols
        split = shape[:axis] + (tensor, pieces, cols) + shape[axis + 1 :]
        return jnp.swapaxes(table.reshape(split), axis, axis + 1).reshape(shape)

    def ungroup(table, axis):
        shape = table.shape
        pieces = units // cols
        split = shape[:axis] + (pieces, tensor, cols) + shape[axis + 1 :]
        return jnp.swapaxes(table.reshape(split), axis, axis + 1).reshape(shape)

    def effective(weight, lower, raised):
        return (weight.astype(F32) + mm(lower, raised)).astype(BF)

    def effective_t(weight_t, lower, raised):
        update = lax.dot_general(
            raised, lower, (((0,), (1,)), ((), ())), preferred_element_type=F32
        )
        return (weight_t.astype(F32) + update).astype(BF)

    ta = (pick(timeattend_lower), pick(timeattend_raise))
    to = (pick(timeoutput_lower), pick(timeoutput_raise))
    tm = (pick(timemixing_lower), pick(timemixing_raise))
    sa = (pick(spaceattend_lower), pick(spaceattend_raise))
    so = (pick(spaceoutput_lower), pick(spaceoutput_raise))
    he = (pick(expand_lower), regroup(pick(expand_raise), 1))
    hr = (regroup(pick(reduce_lower), 0), pick(reduce_raise))

    w_ta = effective(wide(time_whole[0:3]), *ta)
    w_to = effective_t(time_whole[3], *to)
    w_tm = effective(time_whole[4], *tm)
    w_sa = effective(wide(rest_whole[0:3]), *sa)
    w_so = effective_t(rest_whole[3], *so)
    w_he = effective(wide(rest_whole[4:8]), *he)
    w_hr = effective_t(wide(rest_whole[8:12]), *hr)

    def low_rank(acts, grad, pair):
        inner = mm(acts, pair[0]).astype(BF)
        inner_grad = mm_t(grad, pair[1]).astype(BF)
        lower_grad = t_mm(inner_grad, acts)
        raised_grad = t_mm(inner, grad)
        return (lower_grad, raised_grad)

    def to_places(values):
        values = values.reshape(frames // tensor, PLACES, width)
        mine = lax.dynamic_slice_in_dim(values, me * half, half, 1)
        other = lax.dynamic_slice_in_dim(values, (1 - me) * half, half, 1)
        got = lax.ppermute(other, "tensor", swap)
        return jnp.concatenate([mine, got], axis=0).reshape(-1, width)

    def to_frames(values):
        values = values.reshape(frames, half, width)
        mine = values[: frames // tensor]
        got = lax.ppermute(values[frames // tensor :], "tensor", swap)
        first = jnp.where(me == 0, mine, got)
        second = jnp.where(me == 0, got, mine)
        return jnp.concatenate([first, second], axis=1).reshape(-1, width)

    frames = frames * tensor
    start = tokens[0].astype(F32)
    start_p = to_places(tokens[0]).astype(F32)
    normed_time = layer_norm(start_p, norm_time).astype(BF)
    packed_time = mm(normed_time, w_ta).astype(BF)
    heads_time, totals_time = attend(packed_time, frames, TIME_FORMS)
    heads_time = heads_time.astype(BF)
    merged_time = mm_t(heads_time, w_to).astype(BF)
    delta = to_frames(mm(merged_time, w_tm).astype(BF))
    local = frames // tensor
    after_time = start + delta.astype(F32)
    normed_space = layer_norm(after_time, norm_space).astype(BF)
    packed_space = mm(normed_space, w_sa).astype(BF)
    heads_space, totals_space = attend(packed_space, local, SPACE_FORMS)
    heads_space = heads_space.astype(BF)
    after_space = after_time + mm_t(heads_space, w_so)
    normed_hidden = layer_norm(after_space, norm_hidden).astype(BF)
    hidden = mm(normed_hidden, w_he)
    active = jax.nn.gelu(hidden, approximate=False).astype(BF)
    layer_output = ((after_space + mm_t(active, w_hr)) * valid).astype(BF)

    upstream = cotangent[0].astype(F32) * valid
    up_low = upstream.astype(BF)
    active_grad = mm(up_low, w_hr)
    g_hr = low_rank(active, up_low, hr)
    _, gelu_back = jax.vjp(partial(jax.nn.gelu, approximate=False), hidden)
    hidden_grad = gelu_back(active_grad)[0].astype(BF)
    g_he = low_rank(normed_hidden, hidden_grad, he)
    _, norm_back = jax.vjp(partial(layer_norm, gain=norm_hidden), after_space)
    space_grad = upstream + norm_back(mm_t(hidden_grad, w_he))[0]
    space_low = space_grad.astype(BF)
    g_so = low_rank(heads_space, space_low, so)
    heads_grad = mm(space_low, w_so).astype(BF)
    packed_grad = attend_back(heads_grad, packed_space, totals_space, local, SPACE_FORMS)
    packed_grad = packed_grad.astype(BF)
    g_sa = low_rank(normed_space, packed_grad, sa)
    _, norm_back = jax.vjp(partial(layer_norm, gain=norm_space), after_time)
    time_grad = space_grad + norm_back(mm_t(packed_grad, w_sa))[0]

    mixing_grad = to_places(time_grad.astype(BF))
    g_tm = low_rank(merged_time, mixing_grad, tm)
    merged_grad = mm_t(mixing_grad, w_tm).astype(BF)
    g_to = low_rank(heads_time, merged_grad, to)
    heads_grad = mm(merged_grad, w_to).astype(BF)
    packed_grad = attend_back(heads_grad, packed_time, totals_time, frames, TIME_FORMS)
    packed_grad = packed_grad.astype(BF)
    g_ta = low_rank(normed_time, packed_grad, ta)
    _, norm_back = jax.vjp(partial(layer_norm, gain=norm_time), start_p)
    first_grad = to_frames(norm_back(mm_t(packed_grad, w_ta))[0].astype(BF))
    input_grad = (time_grad + first_grad.astype(F32)).astype(BF)

    def reduce_tables(pieces):
        flat = jnp.concatenate([piece.astype(BF).reshape(-1) for piece in pieces])
        each = flat.size // devices
        label = jnp.full((devices, 128), adapter, jnp.int32).astype(BF)
        sent = jnp.concatenate([flat.reshape(devices, each), label], axis=1)
        got = lax.all_to_all(sent, ALL, 0, 0, tiled=True)
        owner = got[:, each : each + 1].astype(jnp.int32)
        choose = (owner == jnp.arange(adapters, dtype=jnp.int32)[None, :]).astype(BF)
        total = t_mm(choose, got[:, :each]).astype(BF)
        whole = lax.all_gather(total, ALL, axis=0, tiled=False)
        whole = whole.transpose(1, 0, 2).reshape(adapters, devices * each)
        parts = []
        at = 0
        for piece in pieces:
            parts.append(whole[:, at : at + piece.size].reshape((adapters,) + piece.shape))
            at += piece.size
        return [part.astype(F32) for part in parts]

    late = reduce_tables([*g_hr, *g_he, *g_so, *g_sa])
    early = reduce_tables([*g_tm, *g_to, *g_ta])

    def lowered(part):
        return jnp.swapaxes(part, 1, 2)

    def threes(part):
        return part.reshape(adapters, rank, 3, width)

    return (
        layer_output[None],
        input_grad[None],
        lowered(early[4]),
        threes(early[5]),
        lowered(early[2]),
        early[3],
        lowered(early[0]),
        early[1],
        lowered(late[6]),
        threes(late[7]),
        lowered(late[4]),
        late[5],
        lowered(late[2]),
        ungroup(late[3], 2),
        lowered(ungroup(late[0], 2)),
        late[1],
    )


def solution(mesh):
    whole = P()
    step = partial(body, dp=mesh.shape["dp"], tensor=mesh.shape["tensor"])
    return jax.shard_map(
        step,
        mesh=mesh,
        in_specs=(
            P("dp", "tensor", None),
            P("dp", "tensor", None),
            P("dp", None, "tensor"),
            P("tensor", "dp"),
            P("dp", None),
            P("dp", None, "tensor"),
            P("tensor", "dp"),
            P("dp", "tensor"),
            P("tensor", "dp"),
        )
        + (whole,) * 17
        + (P("dp"), P("dp")),
        out_specs=(P("dp", "tensor", None), P("dp", "tensor", None)) + (whole,) * 14,
        check_vma=False,
    )
```

```python
from functools import partial
import jax
import jax.numpy as jnp
from jax import lax
from jax.experimental import pallas as pl
from jax.experimental.pallas import tpu as pltpu
from jax.sharding import PartitionSpec as P

BF = jnp.bfloat16
F32 = jnp.float32
HEAD = 64
PLACES = 196
LOW = -1e30


def mm(a, b):
    return lax.dot_general(a, b, (((1,), (0,)), ((), ())), preferred_element_type=F32)


def mm_t(a, b):
    return lax.dot_general(a, b, (((1,), (1,)), ((), ())), preferred_element_type=F32)


def t_mm(a, b):
    return lax.dot_general(a, b, (((0,), (0,)), ((), ())), preferred_element_type=F32)


def norm_parts(x):
    center = jnp.mean(x, axis=-1, keepdims=True)
    offset = x - center
    spread = jnp.mean(offset * offset, axis=-1, keepdims=True)
    root = lax.rsqrt(spread + 1e-06)
    return (offset * root, root)


def norm_back(grad, x, gain):
    unit, root = norm_parts(x)
    grad = grad * gain
    first = jnp.mean(grad, axis=-1, keepdims=True)
    second = jnp.mean(grad * unit, axis=-1, keepdims=True)
    return root * (grad - first - unit * second)


def two_heads(x):
    lane = lax.broadcasted_iota(jnp.int32, x.shape, 1)
    zero = jnp.zeros_like(x)
    return jnp.concatenate([jnp.where(lane < HEAD, x, zero), jnp.where(lane < HEAD, zero, x)], axis=0)


def one_pair(x):
    size = x.shape[0] // 2
    lane = lax.broadcasted_iota(jnp.int32, (size, x.shape[1]), 1)
    return jnp.where(lane < HEAD, x[:size], x[size:])


def attend(query, keys, values, bias):
    size = keys.shape[0]
    scores = mm_t(two_heads(keys), query).reshape(2, size, size) + bias[None]
    top = jnp.max(scores, axis=1, keepdims=True)
    parts = jnp.exp(scores - top)
    total = jnp.sum(parts, axis=1, keepdims=True)
    probs = (parts * (1.0 / total)).reshape(2 * size, size).astype(BF)
    mixed = t_mm(two_heads(values), probs)
    return (probs, mixed.T.astype(BF))


def attend_back(grad, query, keys, values, probs):
    size = keys.shape[0]
    prob_grad = mm_t(two_heads(values), grad)
    value_grad = one_pair(mm(probs, grad))
    wide = probs.astype(F32)
    mass = wide * prob_grad
    total = jnp.sum(mass.reshape(2, size, size), axis=1, keepdims=True)
    score_grad = mass - (wide.reshape(2, size, size) * total).reshape(2 * size, size)
    score_grad = score_grad.astype(BF)
    key_grad = one_pair(mm(score_grad, query))
    query_grad = t_mm(two_heads(keys), score_grad).T * HEAD ** (-0.5)
    return (query_grad.astype(BF), key_grad.astype(BF), value_grad.astype(BF))


def split_lanes(ref, base, value):
    for lane in range(value.shape[-1] // 128):
        ref[base + lane] = value[..., lane * 128 : lane * 128 + 128]


def join_lanes(ref, base, count):
    return jnp.concatenate([ref[base + lane] for lane in range(count)], axis=-1)


def gelu_parts(hidden):
    cdf = 0.5 * (1.0 + lax.erf(hidden * 0.7071067811865476))
    density = jnp.exp(-0.5 * hidden * hidden) * 0.3989422804014327
    return (hidden * cdf, cdf + hidden * density)


def space_kernel(
    tokens, delta, cot, valid, gain_s, gain_h, units, gathered,
    out, tgrad, tlow, grads,
    w, x, up, ys, n_lo, qkv, dqkv, probs, att, acc, dacc, gacc, bias, sems,
    *, places, pad,
):
    step = pl.program_id(0)
    nd, nt, count, wr, wc = gathered.shape
    width = nt * wc
    chunk = tokens.shape[0]
    rows = chunk * pad
    lanes = width // 128

    def copies(s):
        return [
            pltpu.make_async_copy(
                gathered.at[:, t, s], w.at[s, :, :, pl.ds(t * wc, wc)], sems.at[s, t]
            )
            for t in range(nt)
        ]

    sides = [(0, 1), (0, 2), (0, 3), (5, 4)] + [(6, 7 + i) for i in range(4)] + [(15, 11 + i) for i in range(4)]

    def slab(s):
        return w[s].reshape(width, width)

    @pl.when(step == 0)
    def _():
        for s in range(count):
            for copy in copies(s):
                copy.start()
        x[:, places:, :] = jnp.zeros((chunk, pad - places, width), F32)
        up[:, places:, :] = jnp.zeros((chunk, pad - places, width), F32)
        key = lax.broadcasted_iota(jnp.int32, (pad, pad), 0)
        bias[...] = jnp.where(key < places, 0.0, LOW)
        gacc[...] = jnp.zeros_like(gacc)
        for s in range(count):
            for copy in copies(s):
                copy.wait()
            a, b = sides[s]
            new = slab(s).astype(F32) + t_mm(units[a], units[b])
            w[s] = new.astype(BF).reshape(w.shape[1:])

    def low_in(acts, unit):
        return mm_t(acts, units[unit]).astype(BF)

    def add_grad(unit, left, right):
        gacc[unit] += t_mm(left, right)

    x[:, :places, :] = tokens[...].astype(F32) + delta[...].astype(F32)
    up[:, :places, :] = cot[...].astype(F32) * valid[0, 0]

    xv = x[...].reshape(rows, width)
    n2 = (norm_parts(xv)[0] * gain_s[...]).astype(BF)
    n_lo[...] = n2
    for s in range(3):
        val = mm(n_lo[...], slab(s))
        if s == 0:
            val = val * HEAD ** (-0.5)
        split_lanes(qkv, s * lanes, val.astype(BF))

    def forward(i, carry):
        f = i // lanes
        hp = i % lanes
        r = pl.ds(f * pad, pad)
        p, o = attend(qkv[hp, r], qkv[lanes + hp, r], qkv[2 * lanes + hp, r], bias[...])
        probs[i] = p
        att[hp, r] = o
        return carry

    lax.fori_loop(0, chunk * lanes, forward, 0, unroll=2)

    heads = join_lanes(att, 0, lanes)
    ys[...] = x[...].reshape(rows, width) + mm_t(heads, slab(3))
    inner_so = low_in(heads, 4)
    n3 = (norm_parts(ys[...])[0] * gain_h[...]).astype(BF)
    n_lo[...] = n3
    inner_he = low_in(n3, 6)
    upl = up[...].reshape(rows, width).astype(BF)
    igrad_hr = mm_t(upl, units[15]).astype(BF)
    acc[...] = jnp.zeros_like(acc)
    dacc[...] = jnp.zeros_like(dacc)

    def feed(j, carry):
        inner_hr, igrad_he = carry
        hidden = mm(n_lo[...], w[4 + j].reshape(width, width))
        active, slope = gelu_parts(hidden)
        active = active.astype(BF)
        upl = up[...].reshape(rows, width).astype(BF)
        hgrad = (mm(upl, w[8 + j].reshape(width, width)) * slope).astype(BF)
        acc[...] += mm_t(active, w[8 + j].reshape(width, width))
        dacc[...] += mm_t(hgrad, w[4 + j].reshape(width, width))
        inner_hr = inner_hr + mm_t(active, units[11 + j])
        igrad_he = igrad_he + mm_t(hgrad, units[7 + j])
        gacc[11 + j] += t_mm(igrad_hr, active)
        gacc[7 + j] += t_mm(inner_he, hgrad)
        return (inner_hr, igrad_he)

    zero = jnp.zeros((rows, units.shape[1]), F32)
    inner_hr, igrad_he = lax.fori_loop(0, 4, feed, (zero, zero))
    add_grad(15, inner_hr.astype(BF), upl)
    add_grad(6, igrad_he.astype(BF), n_lo[...])

    res = (ys[...] + acc[...]) * valid[0, 0]
    out[...] = res.reshape(chunk, pad, width)[:, :places].astype(BF)
    sg = up[...].reshape(rows, width) + norm_back(dacc[...], ys[...], gain_h[...])
    acc[...] = sg
    sgl = sg.astype(BF)
    heads = join_lanes(att, 0, lanes)
    igrad = low_in(sgl, 5)
    add_grad(4, igrad, heads)
    add_grad(5, inner_so, sgl)
    split_lanes(att, 0, mm(sgl, slab(3)).astype(BF))

    def backward(i, carry):
        f = i // lanes
        hp = i % lanes
        r = pl.ds(f * pad, pad)
        dq, dk, dv = attend_back(
            att[hp, r], qkv[hp, r], qkv[lanes + hp, r], qkv[2 * lanes + hp, r], probs[i]
        )
        dqkv[hp, r] = dq
        dqkv[lanes + hp, r] = dk
        dqkv[2 * lanes + hp, r] = dv
        return carry

    lax.fori_loop(0, chunk * lanes, backward, 0, unroll=2)

    n2 = (norm_parts(x[...].reshape(rows, width))[0] * gain_s[...]).astype(BF)
    inner_sa = low_in(n2, 0)
    dn = jnp.zeros((rows, width), F32)
    igrad = jnp.zeros((rows, units.shape[1]), F32)
    for s in range(3):
        g = join_lanes(dqkv, s * lanes, lanes)
        dn = dn + mm_t(g, slab(s))
        igrad = igrad + mm_t(g, units[1 + s])
        add_grad(1 + s, inner_sa, g)
    add_grad(0, igrad.astype(BF), n2)
    tg = acc[...] + norm_back(dn, x[...].reshape(rows, width), gain_s[...])
    tg = tg.reshape(chunk, pad, width)[:, :places]
    tgrad[...] = tg
    tlow[...] = tg.astype(BF)

    @pl.when(step == pl.num_programs(0) - 1)
    def _():
        n, rank, _ = gacc.shape
        for c in range(lanes):
            grads[c] = gacc[:, :, c * 128 : c * 128 + 128].reshape(n * rank, 128).astype(BF)


def space_call(tokens, delta, cot, valid, gain_s, gain_h, units, gathered, chunk=2):
    frames, places, width = tokens.shape
    pad = -(-places // 16) * 16
    rows = chunk * pad
    nd, nt, count, wr, wc = gathered.shape
    n, rank, _ = units.shape
    lanes = width // 128
    block = pl.BlockSpec((chunk, places, width), lambda i: (i, 0, 0))
    full = lambda a: pl.BlockSpec(a.shape, lambda i: (0,) * a.ndim, pipeline_mode=pl.Buffered(1))
    return pl.pallas_call(
        partial(space_kernel, places=places, pad=pad),
        grid=(frames // chunk,),
        out_shape=(
            jax.ShapeDtypeStruct(tokens.shape, BF),
            jax.ShapeDtypeStruct(tokens.shape, F32),
            jax.ShapeDtypeStruct(tokens.shape, BF),
            jax.ShapeDtypeStruct((lanes, n * rank, 128), BF),
        ),
        in_specs=[
            block, block, block,
            pl.BlockSpec(memory_space=pltpu.SMEM),
            full(gain_s), full(gain_h), full(units),
            pl.BlockSpec(memory_space=pl.ANY),
        ],
        out_specs=(block, block, block, pl.BlockSpec((lanes, n * rank, 128), lambda i: (0, 0, 0))),
        scratch_shapes=[
            pltpu.VMEM((count, nd, wr, width), BF),
            pltpu.VMEM((chunk, pad, width), F32),
            pltpu.VMEM((chunk, pad, width), F32),
            pltpu.VMEM((rows, width), F32),
            pltpu.VMEM((rows, width), BF),
            pltpu.VMEM((3 * lanes, rows, 128), BF),
            pltpu.VMEM((3 * lanes, rows, 128), BF),
            pltpu.VMEM((chunk * lanes, 2 * pad, pad), BF),
            pltpu.VMEM((lanes, rows, 128), BF),
            pltpu.VMEM((rows, width), F32),
            pltpu.VMEM((rows, width), F32),
            pltpu.VMEM((n, rank, width), F32),
            pltpu.VMEM((pad, pad), F32),
            pltpu.SemaphoreType.DMA((count, nt)),
        ],
        compiler_params=pltpu.CompilerParams(
            dimension_semantics=("arbitrary",), vmem_limit_bytes=60 << 20
        ),
    )(tokens, delta, cot, valid, gain_s, gain_h, units, gathered)


TIME_SIDES = ((0, 1), (0, 2), (0, 3), (5, 4), (6, 7))


def load_weights(gathered, w, sems, units, sides):
    nd, nt, count, wr, wc = gathered.shape
    width = nt * wc
    moves = [
        [
            pltpu.make_async_copy(
                gathered.at[:, t, s], w.at[s, :, :, pl.ds(t * wc, wc)], sems.at[s, t]
            )
            for t in range(nt)
        ]
        for s in range(count)
    ]
    for pair in moves:
        for move in pair:
            move.start()
    for s in range(count):
        for move in moves[s]:
            move.wait()
        a, b = sides[s]
        new = w[s].reshape(width, width).astype(F32) + t_mm(units[a], units[b])
        w[s] = new.astype(BF).reshape(w.shape[1:])


def place_bias(bias, group):
    key = lax.broadcasted_iota(jnp.int32, bias.shape, 0)
    query = lax.broadcasted_iota(jnp.int32, bias.shape, 1)
    bias[...] = jnp.where(lax.rem(key, group) == lax.rem(query, group), 0.0, LOW)


def time_kernel(
    mine, got, gain, units, gathered,
    delta, qkv, probs, att, tout, w,
    x, n_lo, bias, sems,
    *, pad, group,
):
    nd, nt, count, wr, wc = gathered.shape
    width = nt * wc
    near, places, _ = mine.shape
    frames = near + got.shape[0]
    lanes = width // 128
    cut = frames // 2
    part = cut * pad
    size = frames * group
    load_weights(gathered, w, sems, units, TIME_SIDES)
    place_bias(bias, group)
    x[:near, :places, :] = mine[...].astype(F32)
    x[near:, :places, :] = got[...].astype(F32)
    x[:, places:, :] = jnp.zeros((frames, pad - places, width), F32)

    def slab(s):
        return w[s].reshape(width, width)

    def project(c, carry):
        r = pl.ds(c * cut, cut)
        n = (norm_parts(x[r].reshape(part, width))[0] * gain[...]).astype(BF)
        n_lo[...] = n
        for s in range(3):
            val = mm(n_lo[...], slab(s))
            if s == 0:
                val = val * HEAD ** (-0.5)
            val = val.astype(BF).reshape(cut, pad, width)
            for lane in range(lanes):
                qkv[s * lanes + lane, r] = val[:, :, lane * 128 : lane * 128 + 128]
        return carry

    lax.fori_loop(0, 2, project, 0)

    def forward(i, carry):
        b = i // lanes
        hp = i % lanes
        r = pl.ds(pl.multiple_of(b * group, group), group)
        q, k, v = [qkv[s * lanes + hp, :, r].reshape(size, 128) for s in range(3)]
        p, o = attend(q, k, v, bias[...])
        probs[i] = p
        att[hp, :, r] = o.reshape(frames, group, 128)
        return carry

    lax.fori_loop(0, (pad // group) * lanes, forward, 0, unroll=3)

    def merge(c, carry):
        r = pl.ds(c * cut, cut)
        heads = jnp.concatenate([att[lane, r].reshape(part, 128) for lane in range(lanes)], axis=-1)
        merged = mm_t(heads, slab(3)).astype(BF)
        tout[r] = merged.reshape(cut, pad, width)
        val = mm(merged, slab(4)).astype(BF)
        delta[r] = val.reshape(cut, pad, width)[:, :places]
        return carry

    lax.fori_loop(0, 2, merge, 0)


def time_call(mine, got, gain, units, gathered, group=16):
    near, places, width = mine.shape
    frames = 2 * near
    pad = -(-places // group) * group
    nd, nt, count, wr, wc = gathered.shape
    lanes = width // 128
    blocks = pad // group
    size = frames * group
    vm = pl.BlockSpec(memory_space=pltpu.VMEM)
    return pl.pallas_call(
        partial(time_kernel, pad=pad, group=group),
        out_shape=(
            jax.ShapeDtypeStruct((frames, places, width), BF),
            jax.ShapeDtypeStruct((3 * lanes, frames, pad, 128), BF),
            jax.ShapeDtypeStruct((blocks * lanes, 2 * size, size), BF),
            jax.ShapeDtypeStruct((lanes, frames, pad, 128), BF),
            jax.ShapeDtypeStruct((frames, pad, width), BF),
            jax.ShapeDtypeStruct((count, nd, wr, width), BF),
        ),
        in_specs=[vm, vm, vm, vm, pl.BlockSpec(memory_space=pl.ANY)],
        out_specs=(vm,) * 6,
        scratch_shapes=[
            pltpu.VMEM((frames, pad, width), F32),
            pltpu.VMEM((frames // 2 * pad, width), BF),
            pltpu.VMEM((size, size), F32),
            pltpu.SemaphoreType.DMA((count, nt)),
        ],
        compiler_params=pltpu.CompilerParams(vmem_limit_bytes=60 << 20),
    )(mine, got, gain, units, gathered)


def time_back_kernel(
    gmine, ggot, mine, got, gain, units, qkv, probs, att, tout, w,
    first, grads,
    x, g_lo, mg, dqkv, gacc,
    *, group,
):
    count, nd, wr, width = w.shape
    near, places, _ = mine.shape
    frames, pad, _ = tout.shape
    lanes = width // 128
    cut = frames // 2
    part = cut * pad
    size = frames * group
    gap = jnp.zeros((frames, pad - places, width), F32)
    x[:near, :places, :] = mine[...].astype(F32)
    x[near:, :places, :] = got[...].astype(F32)
    x[:, places:, :] = gap
    g_lo[:near, :places, :] = gmine[...]
    g_lo[near:, :places, :] = ggot[...]
    g_lo[:, places:, :] = gap.astype(BF)
    gacc[...] = jnp.zeros_like(gacc)

    def slab(s):
        return w[s].reshape(width, width)

    def flat(ref, r):
        return ref[r].reshape(part, width)

    def lane_rows(ref, base, r):
        return jnp.concatenate(
            [ref[base + lane, r].reshape(part, 128) for lane in range(lanes)], axis=-1
        )

    def outer(c, carry):
        r = pl.ds(c * cut, cut)
        g = flat(g_lo, r)
        merged = flat(tout, r)
        inner = mm_t(merged, units[6]).astype(BF)
        igrad = mm_t(g, units[7]).astype(BF)
        gacc[6] += t_mm(igrad, merged)
        gacc[7] += t_mm(inner, g)
        grad = mm_t(g, slab(4)).astype(BF)
        heads = lane_rows(att, 0, r)
        inner = mm_t(heads, units[4]).astype(BF)
        igrad = mm_t(grad, units[5]).astype(BF)
        gacc[4] += t_mm(igrad, heads)
        gacc[5] += t_mm(inner, grad)
        val = mm(grad, slab(3)).astype(BF).reshape(cut, pad, width)
        for lane in range(lanes):
            mg[lane, r] = val[:, :, lane * 128 : lane * 128 + 128]
        return carry

    lax.fori_loop(0, 2, outer, 0)

    def backward(i, carry):
        b = i // lanes
        hp = i % lanes
        r = pl.ds(pl.multiple_of(b * group, group), group)
        q, k, v = [qkv[s * lanes + hp, :, r].reshape(size, 128) for s in range(3)]
        g = mg[hp, :, r].reshape(size, 128)
        for s, val in enumerate(attend_back(g, q, k, v, probs[i])):
            dqkv[s * lanes + hp, :, r] = val.reshape(frames, group, 128)
        return carry

    lax.fori_loop(0, (pad // group) * lanes, backward, 0, unroll=3)

    def inner_part(c, carry):
        r = pl.ds(c * cut, cut)
        xv = flat(x, r)
        n = (norm_parts(xv)[0] * gain[...]).astype(BF)
        inner = mm_t(n, units[0]).astype(BF)
        dn = jnp.zeros((part, width), F32)
        igrad = jnp.zeros((part, units.shape[1]), F32)
        for s in range(3):
            g = lane_rows(dqkv, s * lanes, r)
            dn = dn + mm_t(g, slab(s))
            igrad = igrad + mm_t(g, units[1 + s])
            gacc[1 + s] += t_mm(inner, g)
        gacc[0] += t_mm(igrad.astype(BF), n)
        val = norm_back(dn, flat(x, r), gain[...]).astype(BF)
        first[r] = val.reshape(cut, pad, width)[:, :places]
        return carry

    lax.fori_loop(0, 2, inner_part, 0)
    n, rank, _ = gacc.shape
    for c in range(lanes):
        grads[c] = gacc[:, :, c * 128 : c * 128 + 128].reshape(n * rank, 128).astype(BF)


def time_back_call(gmine, ggot, mine, got, gain, units, qkv, probs, att, tout, w, group=16):
    near, places, width = mine.shape
    frames, pad, _ = tout.shape
    lanes = width // 128
    n, rank, _ = units.shape
    vm = pl.BlockSpec(memory_space=pltpu.VMEM)
    return pl.pallas_call(
        partial(time_back_kernel, group=group),
        out_shape=(
            jax.ShapeDtypeStruct((frames, places, width), BF),
            jax.ShapeDtypeStruct((lanes, n * rank, 128), BF),
        ),
        in_specs=[vm] * 11,
        out_specs=(vm, vm),
        scratch_shapes=[
            pltpu.VMEM((frames, pad, width), F32),
            pltpu.VMEM((frames, pad, width), BF),
            pltpu.VMEM((lanes, frames, pad, 128), BF),
            pltpu.VMEM((3 * lanes, frames, pad, 128), BF),
            pltpu.VMEM((n, rank, width), F32),
        ],
        compiler_params=pltpu.CompilerParams(vmem_limit_bytes=60 << 20),
    )(gmine, ggot, mine, got, gain, units, qkv, probs, att, tout, w)


ALL = ("dp", "tensor")


def body(
    tokens,
    cotangent,
    time_attend,
    time_output,
    time_mixing,
    space_attend,
    space_output,
    hidden_expand,
    hidden_reduce,
    norm_time,
    norm_space,
    norm_hidden,
    timeattend_lower,
    timeattend_raise,
    timeoutput_lower,
    timeoutput_raise,
    timemixing_lower,
    timemixing_raise,
    spaceattend_lower,
    spaceattend_raise,
    spaceoutput_lower,
    spaceoutput_raise,
    expand_lower,
    expand_raise,
    reduce_lower,
    reduce_raise,
    adapter_index,
    clip_mask,
    *,
    dp,
    tensor,
):
    me = lax.axis_index("tensor")
    devices = dp * tensor
    _, length, width = tokens.shape
    local = length // PLACES
    half = PLACES // tensor
    adapters, _, rank = timeattend_lower.shape
    cols = width // tensor
    pieces = hidden_expand.shape[1] // cols
    lanes = width // 128
    adapter = adapter_index[0]
    valid = clip_mask.astype(F32).reshape(1, 1)
    swap = [(i, (i + 1) % tensor) for i in range(tensor)]

    def slabs(matrix):
        return matrix.reshape(matrix.shape[0], -1, cols).transpose(1, 0, 2)

    def gather(pack):
        whole = lax.all_gather(pack, ALL, axis=0, tiled=False)
        count, rows, _ = pack.shape
        whole = whole.reshape(dp, tensor, count, rows, cols)
        if rows % 16:
            whole = whole.transpose(2, 0, 3, 1, 4).reshape(1, 1, count, width, width)
        return whole

    mixing_cols = lax.dynamic_slice_in_dim(time_mixing, me * cols, cols, 1)
    time_pack = [slabs(time_attend), slabs(time_output.T), slabs(mixing_cols)]
    rest_pack = [
        slabs(space_attend),
        slabs(space_output.T),
        slabs(hidden_expand),
        slabs(hidden_reduce.T),
    ]
    time_whole = gather(jnp.concatenate(time_pack, axis=0))
    rest_whole = gather(jnp.concatenate(rest_pack, axis=0))

    def pick(table):
        return lax.dynamic_index_in_dim(table, adapter, 0, keepdims=False)

    def lower(table):
        picked = pick(table)
        if picked.shape[0] == width:
            return picked.T[None]
        split = picked.reshape(tensor, pieces, cols, rank)
        return split.transpose(1, 3, 0, 2).reshape(pieces, rank, width)

    def raised(table):
        picked = pick(table)
        if picked.ndim == 3:
            return picked.transpose(1, 0, 2)
        if picked.shape[1] == width:
            return picked[None]
        split = picked.reshape(rank, tensor, pieces, cols)
        return split.transpose(2, 0, 1, 3).reshape(pieces, rank, width)

    time_tables = [
        lower(timeattend_lower),
        raised(timeattend_raise),
        lower(timeoutput_lower),
        raised(timeoutput_raise),
        lower(timemixing_lower),
        raised(timemixing_raise),
    ]
    rest_tables = [
        lower(spaceattend_lower),
        raised(spaceattend_raise),
        lower(spaceoutput_lower),
        raised(spaceoutput_raise),
        lower(expand_lower),
        raised(expand_raise),
        lower(reduce_lower),
        raised(reduce_raise),
    ]
    time_units = jnp.concatenate(time_tables, axis=0)
    rest_units = jnp.concatenate(rest_tables, axis=0)

    def to_places(values):
        mine = lax.dynamic_slice_in_dim(values, me * half, half, 1)
        other = lax.dynamic_slice_in_dim(values, (1 - me) * half, half, 1)
        return (mine, lax.ppermute(other, "tensor", swap))

    def to_frames(values):
        mine = values[:local]
        got = lax.ppermute(values[local:], "tensor", swap)
        first = jnp.where(me == 0, mine, got)
        second = jnp.where(me == 0, got, mine)
        return jnp.concatenate([first, second], axis=1)

    tokens = tokens.reshape(local, PLACES, width)
    cotangent = cotangent.reshape(local, PLACES, width)
    gains = [gain.reshape(1, width) for gain in (norm_time, norm_space, norm_hidden)]
    mine, got = to_places(tokens)
    delta, *kept = time_call(mine, got, gains[0], time_units, time_whole)
    layer_output, time_grad, time_low, late = space_call(
        tokens, to_frames(delta), cotangent, valid, gains[1], gains[2], rest_units, rest_whole
    )
    first, early = time_back_call(*to_places(time_low), mine, got, gains[0], time_units, *kept)
    input_grad = (time_grad + to_frames(first).astype(F32)).astype(BF)

    def reduce_tables(sums):
        flat = sums.reshape(-1, 128)
        each = flat.shape[0] // devices
        label = jnp.full((devices, 1, 128), adapter, jnp.int32).astype(BF)
        sent = jnp.concatenate([flat.reshape(devices, each, 128), label], axis=1)
        back = lax.all_to_all(sent, ALL, 0, 0, tiled=True)
        owner = back[:, each, :1].astype(jnp.int32)
        choose = (owner == jnp.arange(adapters, dtype=jnp.int32)[None, :]).astype(BF)
        total = lax.dot_general(
            choose, back[:, :each], (((0,), (0,)), ((), ())), preferred_element_type=F32
        )
        whole = lax.all_gather(total.astype(BF), ALL, axis=0, tiled=False)
        whole = whole.transpose(1, 0, 2, 3)
        return whole.reshape(adapters, lanes, -1, rank, 128)

    late = reduce_tables(late)
    early = reduce_tables(early)

    def lowered(part):
        if part.shape[2] == 1:
            return part[:, :, 0].transpose(0, 1, 3, 2).reshape(adapters, width, rank).astype(F32)
        whole = part.transpose(0, 3, 2, 1, 4).reshape(adapters, rank, pieces, tensor, cols)
        return whole.transpose(0, 3, 2, 4, 1).reshape(adapters, -1, rank).astype(F32)

    def wide(part):
        whole = part.transpose(0, 3, 2, 1, 4).reshape(adapters, rank, -1, width)
        return whole.astype(F32)

    def row(part):
        return wide(part).reshape(adapters, rank, width)

    expand = wide(late[:, :, 7:11]).reshape(adapters, rank, pieces, tensor, cols)
    expand = expand.transpose(0, 1, 3, 2, 4).reshape(adapters, rank, -1)
    return (
        layer_output.reshape(1, length, width),
        input_grad.reshape(1, length, width),
        lowered(early[:, :, 0:1]),
        wide(early[:, :, 1:4]),
        lowered(early[:, :, 4:5]),
        row(early[:, :, 5:6]),
        lowered(early[:, :, 6:7]),
        row(early[:, :, 7:8]),
        lowered(late[:, :, 0:1]),
        wide(late[:, :, 1:4]),
        lowered(late[:, :, 4:5]),
        row(late[:, :, 5:6]),
        lowered(late[:, :, 6:7]),
        expand,
        lowered(late[:, :, 11:15]),
        row(late[:, :, 15:16]),
    )


def solution(mesh):
    whole = P()
    step = partial(body, dp=mesh.shape["dp"], tensor=mesh.shape["tensor"])
    return jax.shard_map(
        step,
        mesh=mesh,
        in_specs=(
            P("dp", "tensor", None),
            P("dp", "tensor", None),
            P("dp", None, "tensor"),
            P("tensor", "dp"),
            P("dp", None),
            P("dp", None, "tensor"),
            P("tensor", "dp"),
            P("dp", "tensor"),
            P("tensor", "dp"),
        )
        + (whole,) * 17
        + (P("dp"), P("dp")),
        out_specs=(P("dp", "tensor", None), P("dp", "tensor", None)) + (whole,) * 14,
        check_vma=False,
    )
```

```python
from functools import partial
import jax
import jax.numpy as jnp
from jax import lax
from jax.experimental import pallas as pl
from jax.experimental.pallas import tpu as pltpu
from jax.sharding import PartitionSpec as P

BF = jnp.bfloat16
F32 = jnp.float32
HEAD = 64
PLACES = 196
LOW = -1e30


def mm(a, b):
    return lax.dot_general(a, b, (((1,), (0,)), ((), ())), preferred_element_type=F32)


def mm_t(a, b):
    return lax.dot_general(a, b, (((1,), (1,)), ((), ())), preferred_element_type=F32)


def t_mm(a, b):
    return lax.dot_general(a, b, (((0,), (0,)), ((), ())), preferred_element_type=F32)


def norm_parts(x):
    center = jnp.mean(x, axis=-1, keepdims=True)
    offset = x - center
    spread = jnp.mean(offset * offset, axis=-1, keepdims=True)
    root = lax.rsqrt(spread + 1e-06)
    return (offset * root, root)


def norm_back(grad, x, gain):
    unit, root = norm_parts(x)
    grad = grad * gain
    first = jnp.mean(grad, axis=-1, keepdims=True)
    second = jnp.mean(grad * unit, axis=-1, keepdims=True)
    return root * (grad - first - unit * second)


def two_heads(x):
    lane = lax.broadcasted_iota(jnp.int32, x.shape, 1)
    zero = jnp.zeros_like(x)
    return jnp.concatenate([jnp.where(lane < HEAD, x, zero), jnp.where(lane < HEAD, zero, x)], axis=0)


def one_pair(x):
    size = x.shape[0] // 2
    lane = lax.broadcasted_iota(jnp.int32, (size, x.shape[1]), 1)
    return jnp.where(lane < HEAD, x[:size], x[size:])


def attend(query, keys, values, bias):
    size = keys.shape[0]
    scores = mm_t(two_heads(keys), query).reshape(2, size, size) + bias[None]
    top = jnp.max(scores, axis=1, keepdims=True)
    parts = jnp.exp(scores - top)
    total = jnp.sum(parts, axis=1, keepdims=True)
    probs = (parts * (1.0 / total)).reshape(2 * size, size).astype(BF)
    mixed = t_mm(two_heads(values), probs)
    return (probs, mixed.T.astype(BF))


def attend_back(grad, query, keys, values, probs):
    size = keys.shape[0]
    prob_grad = mm_t(two_heads(values), grad)
    value_grad = one_pair(mm(probs, grad))
    wide = probs.astype(F32)
    mass = wide * prob_grad
    total = jnp.sum(mass.reshape(2, size, size), axis=1, keepdims=True)
    score_grad = mass - (wide.reshape(2, size, size) * total).reshape(2 * size, size)
    score_grad = score_grad.astype(BF)
    key_grad = one_pair(mm(score_grad, query))
    query_grad = t_mm(two_heads(keys), score_grad).T * HEAD ** (-0.5)
    return (query_grad.astype(BF), key_grad.astype(BF), value_grad.astype(BF))


def split_lanes(ref, base, value):
    for lane in range(value.shape[-1] // 128):
        ref[base + lane] = value[..., lane * 128 : lane * 128 + 128]


def join_lanes(ref, base, count):
    return jnp.concatenate([ref[base + lane] for lane in range(count)], axis=-1)


def gelu_parts(hidden):
    cdf = 0.5 * (1.0 + lax.erf(hidden * 0.7071067811865476))
    density = jnp.exp(-0.5 * hidden * hidden) * 0.3989422804014327
    return (hidden * cdf, cdf + hidden * density)


def space_kernel(
    tokens, near, far, cot, valid, me, gain_s, gain_h, units, gathered,
    out, tgrad, keep, send, grads,
    w, x, up, ys, n_lo, qkv, dqkv, probs, att, acc, dacc, gacc, bias, sems,
    *, places, pad,
):
    step = pl.program_id(0)
    nd, nt, count, wr, wc = gathered.shape
    width = nt * wc
    chunk = tokens.shape[0]
    rows = chunk * pad
    lanes = width // 128

    def copies(s):
        return [
            pltpu.make_async_copy(
                gathered.at[:, t, s], w.at[s, :, :, pl.ds(t * wc, wc)], sems.at[s, t]
            )
            for t in range(nt)
        ]

    sides = [(0, 1), (0, 2), (0, 3), (5, 4)] + [(6, 7 + i) for i in range(4)] + [(15, 11 + i) for i in range(4)]

    def slab(s):
        return w[s].reshape(width, width)

    @pl.when(step == 0)
    def _():
        for s in range(count):
            for copy in copies(s):
                copy.start()
        x[:, places:, :] = jnp.zeros((chunk, pad - places, width), F32)
        up[:, places:, :] = jnp.zeros((chunk, pad - places, width), F32)
        key = lax.broadcasted_iota(jnp.int32, (pad, pad), 0)
        bias[...] = jnp.where(key < places, 0.0, LOW)
        gacc[...] = jnp.zeros_like(gacc)
        for s in range(count):
            for copy in copies(s):
                copy.wait()
            a, b = sides[s]
            new = slab(s).astype(F32) + t_mm(units[a], units[b])
            w[s] = new.astype(BF).reshape(w.shape[1:])

    def low_in(acts, unit):
        return mm_t(acts, units[unit]).astype(BF)

    def add_grad(unit, left, right):
        gacc[unit] += t_mm(left, right)

    half = places // 2
    first = me[0, 0] == 0
    lead = jnp.where(first, near[...], far[...]).astype(F32)
    rest = jnp.where(first, far[...], near[...]).astype(F32)
    x[:, :places, :] = tokens[...].astype(F32) + jnp.concatenate([lead, rest], axis=1)
    up[:, :places, :] = cot[...].astype(F32) * valid[0, 0]

    xv = x[...].reshape(rows, width)
    n2 = (norm_parts(xv)[0] * gain_s[...]).astype(BF)
    n_lo[...] = n2
    for s in range(3):
        val = mm(n_lo[...], slab(s))
        if s == 0:
            val = val * HEAD ** (-0.5)
        split_lanes(qkv, s * lanes, val.astype(BF))

    def forward(i, carry):
        f = i // lanes
        hp = i % lanes
        r = pl.ds(f * pad, pad)
        p, o = attend(qkv[hp, r], qkv[lanes + hp, r], qkv[2 * lanes + hp, r], bias[...])
        probs[i] = p
        att[hp, r] = o
        return carry

    lax.fori_loop(0, chunk * lanes, forward, 0, unroll=4)

    heads = join_lanes(att, 0, lanes)
    ys[...] = x[...].reshape(rows, width) + mm_t(heads, slab(3))
    inner_so = low_in(heads, 4)
    n3 = (norm_parts(ys[...])[0] * gain_h[...]).astype(BF)
    n_lo[...] = n3
    inner_he = low_in(n3, 6)
    upl = up[...].reshape(rows, width).astype(BF)
    igrad_hr = mm_t(upl, units[15]).astype(BF)
    acc[...] = jnp.zeros_like(acc)
    dacc[...] = jnp.zeros_like(dacc)

    def feed(j, carry):
        inner_hr, igrad_he = carry
        hidden = mm(n_lo[...], w[4 + j].reshape(width, width))
        active, slope = gelu_parts(hidden)
        active = active.astype(BF)
        upl = up[...].reshape(rows, width).astype(BF)
        hgrad = (mm(upl, w[8 + j].reshape(width, width)) * slope).astype(BF)
        acc[...] += mm_t(active, w[8 + j].reshape(width, width))
        dacc[...] += mm_t(hgrad, w[4 + j].reshape(width, width))
        inner_hr = inner_hr + mm_t(active, units[11 + j])
        igrad_he = igrad_he + mm_t(hgrad, units[7 + j])
        gacc[11 + j] += t_mm(igrad_hr, active)
        gacc[7 + j] += t_mm(inner_he, hgrad)
        return (inner_hr, igrad_he)

    zero = jnp.zeros((rows, units.shape[1]), F32)
    inner_hr, igrad_he = lax.fori_loop(0, 4, feed, (zero, zero))
    add_grad(15, inner_hr.astype(BF), upl)
    add_grad(6, igrad_he.astype(BF), n_lo[...])

    res = (ys[...] + acc[...]) * valid[0, 0]
    out[...] = res.reshape(chunk, pad, width)[:, :places].astype(BF)
    sg = up[...].reshape(rows, width) + norm_back(dacc[...], ys[...], gain_h[...])
    acc[...] = sg
    sgl = sg.astype(BF)
    heads = join_lanes(att, 0, lanes)
    igrad = low_in(sgl, 5)
    add_grad(4, igrad, heads)
    add_grad(5, inner_so, sgl)
    split_lanes(att, 0, mm(sgl, slab(3)).astype(BF))

    def backward(i, carry):
        f = i // lanes
        hp = i % lanes
        r = pl.ds(f * pad, pad)
        dq, dk, dv = attend_back(
            att[hp, r], qkv[hp, r], qkv[lanes + hp, r], qkv[2 * lanes + hp, r], probs[i]
        )
        dqkv[hp, r] = dq
        dqkv[lanes + hp, r] = dk
        dqkv[2 * lanes + hp, r] = dv
        return carry

    lax.fori_loop(0, chunk * lanes, backward, 0, unroll=4)

    n2 = (norm_parts(x[...].reshape(rows, width))[0] * gain_s[...]).astype(BF)
    inner_sa = low_in(n2, 0)
    dn = jnp.zeros((rows, width), F32)
    igrad = jnp.zeros((rows, units.shape[1]), F32)
    for s in range(3):
        g = join_lanes(dqkv, s * lanes, lanes)
        dn = dn + mm_t(g, slab(s))
        igrad = igrad + mm_t(g, units[1 + s])
        add_grad(1 + s, inner_sa, g)
    add_grad(0, igrad.astype(BF), n2)
    tg = acc[...] + norm_back(dn, x[...].reshape(rows, width), gain_s[...])
    tg = tg.reshape(chunk, pad, width)[:, :places]
    tgrad[...] = tg
    lead = tg[:, :half]
    rest = tg[:, half:]
    keep[...] = jnp.where(first, lead, rest).astype(BF)
    send[...] = jnp.where(first, rest, lead).astype(BF)

    @pl.when(step == pl.num_programs(0) - 1)
    def _():
        n, rank, _ = gacc.shape
        for c in range(lanes):
            grads[c] = gacc[:, :, c * 128 : c * 128 + 128].reshape(n * rank, 128).astype(BF)


def space_call(tokens, near, far, cot, valid, me, gain_s, gain_h, units, gathered, chunk=2):
    frames, places, width = tokens.shape
    pad = -(-places // 16) * 16
    rows = chunk * pad
    nd, nt, count, wr, wc = gathered.shape
    n, rank, _ = units.shape
    lanes = width // 128
    block = pl.BlockSpec((chunk, places, width), lambda i: (i, 0, 0))
    part = pl.BlockSpec((chunk, places // 2, width), lambda i: (i, 0, 0))
    smem = pl.BlockSpec(memory_space=pltpu.SMEM)
    full = lambda a: pl.BlockSpec(a.shape, lambda i: (0,) * a.ndim, pipeline_mode=pl.Buffered(1))
    return pl.pallas_call(
        partial(space_kernel, places=places, pad=pad),
        grid=(frames // chunk,),
        out_shape=(
            jax.ShapeDtypeStruct(tokens.shape, BF),
            jax.ShapeDtypeStruct(tokens.shape, F32),
            jax.ShapeDtypeStruct(near.shape, BF),
            jax.ShapeDtypeStruct(near.shape, BF),
            jax.ShapeDtypeStruct((lanes, n * rank, 128), BF),
        ),
        in_specs=[
            block, part, part, block, smem, smem,
            full(gain_s), full(gain_h), full(units),
            pl.BlockSpec(memory_space=pl.ANY),
        ],
        out_specs=(
            block, block, part, part,
            pl.BlockSpec((lanes, n * rank, 128), lambda i: (0, 0, 0)),
        ),
        scratch_shapes=[
            pltpu.VMEM((count, nd, wr, width), BF),
            pltpu.VMEM((chunk, pad, width), F32),
            pltpu.VMEM((chunk, pad, width), F32),
            pltpu.VMEM((rows, width), F32),
            pltpu.VMEM((rows, width), BF),
            pltpu.VMEM((3 * lanes, rows, 128), BF),
            pltpu.VMEM((3 * lanes, rows, 128), BF),
            pltpu.VMEM((chunk * lanes, 2 * pad, pad), BF),
            pltpu.VMEM((lanes, rows, 128), BF),
            pltpu.VMEM((rows, width), F32),
            pltpu.VMEM((rows, width), F32),
            pltpu.VMEM((n, rank, width), F32),
            pltpu.VMEM((pad, pad), F32),
            pltpu.SemaphoreType.DMA((count, nt)),
        ],
        compiler_params=pltpu.CompilerParams(
            dimension_semantics=("arbitrary",), vmem_limit_bytes=60 << 20
        ),
    )(tokens, near, far, cot, valid, me, gain_s, gain_h, units, gathered)


TIME_SIDES = ((0, 1), (0, 2), (0, 3), (5, 4), (6, 7))


def load_weights(parts, where, w, sems, units, sides):
    count, nd, wr, width = w.shape
    moves = []
    for i, part in enumerate(parts):
        if len(parts) == 1:
            wc = part.shape[4]
            for t in range(part.shape[1]):
                for s in range(count):
                    lane = pl.ds(t * wc, wc)
                    moves.append((part.at[:, t, s], w.at[s, :, :, lane], sems.at[s, t]))
            continue
        planes, turns, _, rows, wc = part.shape
        row = pl.ds(rows * (i % 2), rows)
        for p in range(planes):
            for k in range(turns):
                at = (i * planes + p) * turns + k
                lane = pl.ds(pl.multiple_of(where[at, 1] * wc, 128), wc)
                target = w.at[:, where[at, 0], row, lane]
                moves.append((part.at[p, k], target, sems.at[i, p * turns + k]))
    moves = [pltpu.make_async_copy(*move) for move in moves]
    for move in moves:
        move.start()
    for move in moves:
        move.wait()
    for s in range(count):
        a, b = sides[s]
        new = w[s].reshape(width, width).astype(F32) + t_mm(units[a], units[b])
        w[s] = new.astype(BF).reshape(w.shape[1:])


def place_bias(bias, group):
    key = lax.broadcasted_iota(jnp.int32, bias.shape, 0)
    query = lax.broadcasted_iota(jnp.int32, bias.shape, 1)
    bias[...] = jnp.where(lax.rem(key, group) == lax.rem(query, group), 0.0, LOW)


def time_kernel(*refs, pad, group, parts):
    mine, got, gain, units, where = refs[:5]
    pieces = refs[5 : 5 + parts]
    near_out, far_out, qkv, probs, att, tout, w, x, n_lo, bias, sems = refs[5 + parts :]
    width = w.shape[3]
    near, places, _ = mine.shape
    frames = near + got.shape[0]
    lanes = width // 128
    cut = frames // 2
    part = cut * pad
    size = frames * group
    load_weights(pieces, where, w, sems, units, TIME_SIDES)
    place_bias(bias, group)
    x[:near, :places, :] = mine[...].astype(F32)
    x[near:, :places, :] = got[...].astype(F32)
    x[:, places:, :] = jnp.zeros((frames, pad - places, width), F32)

    def slab(s):
        return w[s].reshape(width, width)

    def project(c, carry):
        r = pl.ds(c * cut, cut)
        n = (norm_parts(x[r].reshape(part, width))[0] * gain[...]).astype(BF)
        n_lo[...] = n
        for s in range(3):
            val = mm(n_lo[...], slab(s))
            if s == 0:
                val = val * HEAD ** (-0.5)
            val = val.astype(BF).reshape(cut, pad, width)
            for lane in range(lanes):
                qkv[s * lanes + lane, r] = val[:, :, lane * 128 : lane * 128 + 128]
        return carry

    lax.fori_loop(0, 2, project, 0)

    def forward(i, carry):
        b = i // lanes
        hp = i % lanes
        r = pl.ds(pl.multiple_of(b * group, group), group)
        q, k, v = [qkv[s * lanes + hp, :, r].reshape(size, 128) for s in range(3)]
        p, o = attend(q, k, v, bias[...])
        probs[i] = p
        att[hp, :, r] = o.reshape(frames, group, 128)
        return carry

    lax.fori_loop(0, (pad // group) * lanes, forward, 0, unroll=6)

    for c, target in ((1, far_out), (0, near_out)):
        r = pl.ds(c * cut, cut)
        heads = jnp.concatenate([att[lane, r].reshape(part, 128) for lane in range(lanes)], axis=-1)
        merged = mm_t(heads, slab(3)).astype(BF)
        tout[r] = merged.reshape(cut, pad, width)
        val = mm(merged, slab(4)).astype(BF)
        target[...] = val.reshape(cut, pad, width)[:, :places]


def time_call(mine, got, gain, units, where, parts, group=16):
    near, places, width = mine.shape
    frames = 2 * near
    pad = -(-places // group) * group
    if len(parts) == 1:
        nd, nt, count, wr, _ = parts[0].shape
        sems = (count, nt)
    else:
        planes, turns, count, wr, _ = parts[0].shape
        nd, wr = len(parts) * planes * turns // 4, 2 * wr
        sems = (len(parts), planes * turns)
    lanes = width // 128
    blocks = pad // group
    size = frames * group
    vm = pl.BlockSpec(memory_space=pltpu.VMEM)
    anywhere = pl.BlockSpec(memory_space=pl.ANY)
    return pl.pallas_call(
        partial(time_kernel, pad=pad, group=group, parts=len(parts)),
        out_shape=(
            jax.ShapeDtypeStruct(mine.shape, BF),
            jax.ShapeDtypeStruct(mine.shape, BF),
            jax.ShapeDtypeStruct((3 * lanes, frames, pad, 128), BF),
            jax.ShapeDtypeStruct((blocks * lanes, 2 * size, size), BF),
            jax.ShapeDtypeStruct((lanes, frames, pad, 128), BF),
            jax.ShapeDtypeStruct((frames, pad, width), BF),
            jax.ShapeDtypeStruct((count, nd, wr, width), BF),
        ),
        in_specs=[vm, vm, vm, vm, pl.BlockSpec(memory_space=pltpu.SMEM)] + [anywhere] * len(parts),
        out_specs=(vm,) * 7,
        scratch_shapes=[
            pltpu.VMEM((frames, pad, width), F32),
            pltpu.VMEM((frames // 2 * pad, width), BF),
            pltpu.VMEM((size, size), F32),
            pltpu.SemaphoreType.DMA(sems),
        ],
        compiler_params=pltpu.CompilerParams(vmem_limit_bytes=60 << 20),
    )(mine, got, gain, units, where, *parts)


def time_back_kernel(
    gmine, ggot, mine, got, gain, units, qkv, probs, att, tout, w,
    near_out, far_out, grads,
    x, g_lo, mg, dqkv, gacc,
    *, group,
):
    count, nd, wr, width = w.shape
    near, places, _ = mine.shape
    frames, pad, _ = tout.shape
    lanes = width // 128
    cut = frames // 2
    part = cut * pad
    size = frames * group
    gap = jnp.zeros((frames, pad - places, width), F32)
    x[:near, :places, :] = mine[...].astype(F32)
    x[near:, :places, :] = got[...].astype(F32)
    x[:, places:, :] = gap
    g_lo[:near, :places, :] = gmine[...]
    g_lo[near:, :places, :] = ggot[...]
    g_lo[:, places:, :] = gap.astype(BF)
    gacc[...] = jnp.zeros_like(gacc)

    def slab(s):
        return w[s].reshape(width, width)

    def flat(ref, r):
        return ref[r].reshape(part, width)

    def lane_rows(ref, base, r):
        return jnp.concatenate(
            [ref[base + lane, r].reshape(part, 128) for lane in range(lanes)], axis=-1
        )

    def outer(c, carry):
        r = pl.ds(c * cut, cut)
        g = flat(g_lo, r)
        merged = flat(tout, r)
        inner = mm_t(merged, units[6]).astype(BF)
        igrad = mm_t(g, units[7]).astype(BF)
        gacc[6] += t_mm(igrad, merged)
        gacc[7] += t_mm(inner, g)
        grad = mm_t(g, slab(4)).astype(BF)
        heads = lane_rows(att, 0, r)
        inner = mm_t(heads, units[4]).astype(BF)
        igrad = mm_t(grad, units[5]).astype(BF)
        gacc[4] += t_mm(igrad, heads)
        gacc[5] += t_mm(inner, grad)
        val = mm(grad, slab(3)).astype(BF).reshape(cut, pad, width)
        for lane in range(lanes):
            mg[lane, r] = val[:, :, lane * 128 : lane * 128 + 128]
        return carry

    lax.fori_loop(0, 2, outer, 0)

    def backward(i, carry):
        b = i // lanes
        hp = i % lanes
        r = pl.ds(pl.multiple_of(b * group, group), group)
        q, k, v = [qkv[s * lanes + hp, :, r].reshape(size, 128) for s in range(3)]
        g = mg[hp, :, r].reshape(size, 128)
        for s, val in enumerate(attend_back(g, q, k, v, probs[i])):
            dqkv[s * lanes + hp, :, r] = val.reshape(frames, group, 128)
        return carry

    lax.fori_loop(0, (pad // group) * lanes, backward, 0, unroll=6)

    for c, target in ((1, far_out), (0, near_out)):
        r = pl.ds(c * cut, cut)
        xv = flat(x, r)
        n = (norm_parts(xv)[0] * gain[...]).astype(BF)
        inner = mm_t(n, units[0]).astype(BF)
        dn = jnp.zeros((part, width), F32)
        igrad = jnp.zeros((part, units.shape[1]), F32)
        for s in range(3):
            g = lane_rows(dqkv, s * lanes, r)
            dn = dn + mm_t(g, slab(s))
            igrad = igrad + mm_t(g, units[1 + s])
            gacc[1 + s] += t_mm(inner, g)
        gacc[0] += t_mm(igrad.astype(BF), n)
        val = norm_back(dn, flat(x, r), gain[...]).astype(BF)
        target[...] = val.reshape(cut, pad, width)[:, :places]

    n, rank, _ = gacc.shape
    for c in range(lanes):
        grads[c] = gacc[:, :, c * 128 : c * 128 + 128].reshape(n * rank, 128).astype(BF)


def time_back_call(gmine, ggot, mine, got, gain, units, qkv, probs, att, tout, w, group=16):
    near, places, width = mine.shape
    frames, pad, _ = tout.shape
    lanes = width // 128
    n, rank, _ = units.shape
    vm = pl.BlockSpec(memory_space=pltpu.VMEM)
    return pl.pallas_call(
        partial(time_back_kernel, group=group),
        out_shape=(
            jax.ShapeDtypeStruct(mine.shape, BF),
            jax.ShapeDtypeStruct(mine.shape, BF),
            jax.ShapeDtypeStruct((lanes, n * rank, 128), BF),
        ),
        in_specs=[vm] * 11,
        out_specs=(vm, vm, vm),
        scratch_shapes=[
            pltpu.VMEM((frames, pad, width), F32),
            pltpu.VMEM((frames, pad, width), BF),
            pltpu.VMEM((lanes, frames, pad, 128), BF),
            pltpu.VMEM((3 * lanes, frames, pad, 128), BF),
            pltpu.VMEM((n, rank, width), F32),
        ],
        compiler_params=pltpu.CompilerParams(vmem_limit_bytes=60 << 20),
    )(gmine, ggot, mine, got, gain, units, qkv, probs, att, tout, w)


def table_kernel(*refs, parts, groups):
    where = refs[0]
    pieces = refs[1 : 1 + parts]
    outs = refs[1 + parts : 1 + parts + len(groups)]
    whole, sems = refs[1 + parts + len(groups) :]
    moves = []
    for i, part in enumerate(pieces):
        if parts == 1:
            moves = [(part.at[d], whole.at[:, d], sems.at[0, d]) for d in range(part.shape[0])]
            continue
        planes, turns, size = part.shape[:3]
        for p in range(planes):
            for k in range(turns):
                at = (i * planes + p) * turns + k
                target = whole.at[pl.ds(size * (i % 2), size), where[at, 0] * 2 + where[at, 1]]
                moves.append((part.at[p, k], target, sems.at[i, p * turns + k]))
    moves = [pltpu.make_async_copy(*move) for move in moves]
    for move in moves:
        move.start()
    for move in moves:
        move.wait()
    adapters, devices, each, _ = whole.shape
    lanes = outs[0].shape[-1] // 128
    rows = devices * each // lanes
    rank = outs[0].shape[-2]

    def one(a, carry):
        flat = whole[a].astype(F32).reshape(devices * each, 128)
        at = 0
        for (count, split), out in zip(groups, outs):
            for u in range(count):
                for c in range(lanes):
                    row = c * rows + (at + u) * rank
                    val = flat[row : row + rank]
                    if split == 0:
                        out[a, u, :, c * 128 : c * 128 + 128] = val
                    else:
                        lane = c * 128 + u * split
                        if c * 128 >= split:
                            lane += (count - 1) * split
                        out[a, :, lane : lane + 128] = val
            at += count
        return carry

    lax.fori_loop(0, adapters, one, 0)


def table_call(where, parts, groups, adapters, rank, width):
    if len(parts) == 1:
        devices, _, each, _ = parts[0].shape
        sems = (1, devices)
    else:
        planes, turns, _, each, _ = parts[0].shape
        devices = len(parts) * planes * turns // 2
        sems = (len(parts), planes * turns)
    shapes = [
        (adapters, count, rank, width) if split == 0 else (adapters, rank, count * width)
        for count, split in groups
    ]
    vm = pl.BlockSpec(memory_space=pltpu.VMEM)
    anywhere = pl.BlockSpec(memory_space=pl.ANY)
    return pl.pallas_call(
        partial(table_kernel, parts=len(parts), groups=tuple(groups)),
        out_shape=[jax.ShapeDtypeStruct(shape, F32) for shape in shapes],
        in_specs=[pl.BlockSpec(memory_space=pltpu.SMEM)] + [anywhere] * len(parts),
        out_specs=[vm] * len(shapes),
        scratch_shapes=[
            pltpu.VMEM((adapters, devices, each, 128), BF),
            pltpu.SemaphoreType.DMA(sems),
        ],
        compiler_params=pltpu.CompilerParams(vmem_limit_bytes=60 << 20),
    )(where, *parts)


ALL = ("dp", "tensor")


def body(
    tokens,
    cotangent,
    time_attend,
    time_output,
    time_mixing,
    space_attend,
    space_output,
    hidden_expand,
    hidden_reduce,
    norm_time,
    norm_space,
    norm_hidden,
    timeattend_lower,
    timeattend_raise,
    timeoutput_lower,
    timeoutput_raise,
    timemixing_lower,
    timemixing_raise,
    spaceattend_lower,
    spaceattend_raise,
    spaceoutput_lower,
    spaceoutput_raise,
    expand_lower,
    expand_raise,
    reduce_lower,
    reduce_raise,
    adapter_index,
    clip_mask,
    *,
    dp,
    tensor,
):
    me = lax.axis_index("tensor")
    devices = dp * tensor
    _, length, width = tokens.shape
    local = length // PLACES
    half = PLACES // tensor
    adapters, _, rank = timeattend_lower.shape
    cols = width // tensor
    pieces = hidden_expand.shape[1] // cols
    lanes = width // 128
    adapter = adapter_index[0]
    valid = clip_mask.astype(F32).reshape(1, 1)
    swap = [(i, (i + 1) % tensor) for i in range(tensor)]

    def slabs(matrix):
        return matrix.reshape(matrix.shape[0], -1, cols).transpose(1, 0, 2)

    tree = dp == 16 and tensor == 2
    spot = lax.axis_index("dp")

    def spread(value, axis):
        def move(piece, pairs, name="dp"):
            return lax.ppermute(piece, name, pairs)

        beside = [(i, i ^ 2) for i in range(dp)]
        cores = [(i, i ^ 1) for i in range(dp)]
        turned = [move(value, [(i, (i + 4 * k) % dp) for i in range(dp)]) for k in range(1, 4)]
        left, right = jnp.split(jnp.stack([value] + turned), 2, axis=axis + 1)
        left = jnp.stack([left, move(left, beside)])
        right = jnp.stack([right, move(right, swap, "tensor")])
        parts = [left, right, move(left, swap, "tensor"), move(right, beside)]
        return parts + [move(part, cores) for part in parts]

    def places_of():
        found = []
        for core in range(2):
            for planes in (((0, 0), (1, 0)), ((0, 0), (0, 1)), ((0, 1), (1, 1)), ((1, 0), (1, 1))):
                for x, t in planes:
                    for k in range(4):
                        base = jnp.bitwise_xor(spot, 2 * x + core)
                        found += [lax.rem(base + dp - 4 * k, dp), jnp.bitwise_xor(me, t)]
        return jnp.stack(found).astype(jnp.int32).reshape(-1, 2)

    where = places_of() if tree else jnp.zeros((1, 2), jnp.int32)

    def gather(pack):
        whole = lax.all_gather(pack, ALL, axis=0, tiled=False)
        count, rows, _ = pack.shape
        whole = whole.reshape(dp, tensor, count, rows, cols)
        if rows % 16:
            whole = whole.transpose(2, 0, 3, 1, 4).reshape(1, 1, count, width, width)
        return whole

    mixing_cols = lax.dynamic_slice_in_dim(time_mixing, me * cols, cols, 1)
    time_pack = [slabs(time_attend), slabs(time_output.T), slabs(mixing_cols)]
    rest_pack = [
        slabs(space_attend),
        slabs(space_output.T),
        slabs(hidden_expand),
        slabs(hidden_reduce.T),
    ]
    time_pack = jnp.concatenate(time_pack, axis=0)
    rest_whole = gather(jnp.concatenate(rest_pack, axis=0))
    time_parts = spread(time_pack, 1) if tree else [gather(time_pack)]

    def pick(table):
        return lax.dynamic_index_in_dim(table, adapter, 0, keepdims=False)

    def lower(table):
        picked = pick(table)
        if picked.shape[0] == width:
            return picked.T[None]
        split = picked.reshape(tensor, pieces, cols, rank)
        return split.transpose(1, 3, 0, 2).reshape(pieces, rank, width)

    def raised(table):
        picked = pick(table)
        if picked.ndim == 3:
            return picked.transpose(1, 0, 2)
        if picked.shape[1] == width:
            return picked[None]
        split = picked.reshape(rank, tensor, pieces, cols)
        return split.transpose(2, 0, 1, 3).reshape(pieces, rank, width)

    time_tables = [
        lower(timeattend_lower),
        raised(timeattend_raise),
        lower(timeoutput_lower),
        raised(timeoutput_raise),
        lower(timemixing_lower),
        raised(timemixing_raise),
    ]
    rest_tables = [
        lower(spaceattend_lower),
        raised(spaceattend_raise),
        lower(spaceoutput_lower),
        raised(spaceoutput_raise),
        lower(expand_lower),
        raised(expand_raise),
        lower(reduce_lower),
        raised(reduce_raise),
    ]
    time_units = jnp.concatenate(time_tables, axis=0)
    rest_units = jnp.concatenate(rest_tables, axis=0)

    def swapped(values):
        return lax.ppermute(values, "tensor", swap)

    tokens = tokens.reshape(local, PLACES, width)
    cotangent = cotangent.reshape(local, PLACES, width)
    gains = [gain.reshape(1, width) for gain in (norm_time, norm_space, norm_hidden)]
    mine = lax.dynamic_slice_in_dim(tokens, me * half, half, 1)
    got = swapped(lax.dynamic_slice_in_dim(tokens, (1 - me) * half, half, 1))
    near, far, *kept = time_call(mine, got, gains[0], time_units, where, time_parts)
    rank_index = me.astype(jnp.int32).reshape(1, 1)
    layer_output, time_grad, keep, send, late = space_call(
        tokens, near, swapped(far), cotangent, valid, rank_index,
        gains[1], gains[2], rest_units, rest_whole,
    )

    def exchange(sums):
        flat = sums.reshape(-1, 128)
        each = flat.shape[0] // devices
        label = jnp.full((devices, 1, 128), adapter, jnp.int32).astype(BF)
        sent = jnp.concatenate([flat.reshape(devices, each, 128), label], axis=1)
        return lax.all_to_all(sent, ALL, 0, 0, tiled=True)

    def combine(back):
        each = back.shape[1] - 1
        owner = back[:, each, :1].astype(jnp.int32)
        choose = (owner == jnp.arange(adapters, dtype=jnp.int32)[None, :]).astype(BF)
        total = lax.dot_general(
            choose, back[:, :each], (((0,), (0,)), ((), ())), preferred_element_type=F32
        )
        return total.astype(BF)

    def gather_sums(total):
        whole = lax.all_gather(total, ALL, axis=0, tiled=False)
        if total.shape[1] % 8:
            whole = whole.transpose(1, 0, 2, 3).reshape(1, adapters, -1, 128)
        return whole

    turned = swapped(send)
    late, keep, turned = lax.optimization_barrier((exchange(late), keep, turned))
    late = gather_sums(combine(late))
    near, far, early = time_back_call(keep, turned, mine, got, gains[0], time_units, *kept)
    early = combine(exchange(early))
    early = spread(early, 0) if tree else [gather_sums(early)]
    got = swapped(far)
    first = jnp.where(me == 0, near, got)
    second = jnp.where(me == 0, got, near)
    first = jnp.concatenate([first, second], axis=1)
    input_grad = (time_grad + first.astype(F32)).astype(BF)

    sizes = (adapters, rank, width)
    late = table_call(
        where, [late], [(1, 0), (3, 0), (1, 0), (1, 0), (1, 0), (pieces, cols), (pieces, cols), (1, 0)],
        *sizes,
    )
    early = table_call(where, early, [(1, 0), (3, 0), (1, 0), (1, 0), (1, 0), (1, 0)], *sizes)

    def lowered(part):
        return part.reshape(adapters, rank, -1).transpose(0, 2, 1)

    def threes(part):
        return part.transpose(0, 2, 1, 3)

    def row(part):
        return part.reshape(adapters, rank, -1)

    return (
        layer_output.reshape(1, length, width),
        input_grad.reshape(1, length, width),
        lowered(early[0]),
        threes(early[1]),
        lowered(early[2]),
        row(early[3]),
        lowered(early[4]),
        row(early[5]),
        lowered(late[0]),
        threes(late[1]),
        lowered(late[2]),
        row(late[3]),
        lowered(late[4]),
        late[5],
        lowered(late[6]),
        row(late[7]),
    )


def solution(mesh):
    whole = P()
    step = partial(body, dp=mesh.shape["dp"], tensor=mesh.shape["tensor"])
    return jax.shard_map(
        step,
        mesh=mesh,
        in_specs=(
            P("dp", "tensor", None),
            P("dp", "tensor", None),
            P("dp", None, "tensor"),
            P("tensor", "dp"),
            P("dp", None),
            P("dp", None, "tensor"),
            P("tensor", "dp"),
            P("dp", "tensor"),
            P("tensor", "dp"),
        )
        + (whole,) * 17
        + (P("dp"), P("dp")),
        out_specs=(P("dp", "tensor", None), P("dp", "tensor", None)) + (whole,) * 14,
        check_vma=False,
    )
```
